256 devices in a mesh: len: 16 (over y, x_lo, core), wid: 16 (over x_hi, z).
Axes of the slice: x: 4 (x_hi: 2, x_lo: 2; x = x_hi * 2 + x_lo), y: 4, z: 8, core: 2. Of those that a mesh axis runs over, the one named last changes fastest.
Arguments:
- ckpt_e: float32 [3, 256, 256, 128], P(None, 'len', 'wid'), may hold values from -6 to 6
- ckpt_h: float32 [3, 256, 256, 128], P(None, 'len', 'wid'), may hold values from -6 to 6
- adj_e: float32 [3, 256, 256, 128], P(None, 'len', 'wid'), may hold values from -6 to 6
- adj_h: float32 [3, 256, 256, 128], P(None, 'len', 'wid'), may hold values from -6 to 6
- material: int32 [256, 256, 128], P('len', 'wid'), may hold values from 0 to 3
- inv_perm: float32 [4], replicated, may hold values from 0.2 to 1
- poling: int32 [32, 32], P('len', 'wid'), may hold values from 0 to 1
- freqs: float32 [8], replicated, may hold values from 0.1 to 3
Outputs:
- adjoint_e: float32 [3, 256, 256, 128], P(None, 'len', 'wid')
- adjoint_h: float32 [3, 256, 256, 128], P(None, 'len', 'wid')
- gradient: float32 [2, 8, 32, 32], P(None, None, 'len', 'wid')
The draws below stay inside these ranges and needn't reach their ends.
All inputs are finite; a program needn't handle non-finite values.
Results may differ from the reference program's by a relative error of at most 0.0001.
Values sent between devices are 32-bit elements; how exact they have to be, the bound alone decides.
No kernel may reach another device: no remote copies, remote signals or barrier semaphores. Data moves between devices by JAX's collectives and lax.ppermute only.
A program may use at most 64 MiB of HBM per device.

```python
import math
import jax
import jax.numpy as jnp
from jax import lax

NZ = 128
STEPS = 8
BINS = 8
NMAT = 4
DOMLEN = 8
WBLK = 8
NX = 256
NY = 256
NDOM = 32
NWB = 32


def touch_ends(drawn, stream_key, least, high):
    shape = drawn.shape
    index_at = [jax.random.randint(jax.random.fold_in(stream_key, axis), (), 0, shape[axis]) for axis in range(len(shape))]
    drawn = drawn.at[tuple(index_at)].set(least)
    longest = shape.index(max(shape))
    index_at[longest] = (index_at[longest] + 1) % shape[longest]
    return drawn.at[tuple(index_at)].set(high)


def block_scale(stream_key, extent, shards, smallest, high):
    level = 1.0
    for position, shards_of in shards:
        draws = jax.random.uniform(jax.random.fold_in(jax.random.fold_in(stream_key, 6), position), (shards_of,), jnp.float32, smallest / len(shards), high / len(shards))
        level = level * jnp.repeat(jnp.exp(draws), extent[position] // shards_of).reshape((-1,) + (1,) * (len(extent) - 1 - position))
    return level


def centred(stream_key, dims, deviation, most, cuts=(), kind=jnp.bfloat16):
    loudness = block_scale(stream_key, dims, cuts, -0.22, 0.18) if cuts else 1.0
    array = jax.random.normal(stream_key, dims, jnp.float32) * deviation * loudness
    return jnp.minimum(jnp.maximum(array, -most), most).astype(kind)


def setup_inputs(seed: int = 0) -> dict:
    splits = jax.random.split(jax.random.key(seed), 9)
    ckpt_e = centred(splits[0], (3, NX, NY, NZ), 1.0, 6.0, ((1, 16), (2, 16)), jnp.float32)
    ckpt_h = centred(splits[1], (3, NX, NY, NZ), 1.0, 6.0, ((1, 16), (2, 16)), jnp.float32)
    adj_e = centred(splits[2], (3, NX, NY, NZ), 1.0, 6.0, ((1, 16), (2, 16)), jnp.float32)
    adj_h = centred(splits[3], (3, NX, NY, NZ), 1.0, 6.0, ((1, 16), (2, 16)), jnp.float32)
    material = touch_ends(jax.random.randint(splits[4], (NX, NY, NZ), 0, NMAT), jax.random.fold_in(splits[4], 1), 0, NMAT - 1).astype(jnp.int32)
    inv_perm = jnp.clip(jax.random.uniform(splits[5], (NMAT,), jnp.float32, 0.2, 1.0), 0.2, 1.0)
    poling = touch_ends(jax.random.randint(splits[6], (NDOM, NWB), 0, 2), jax.random.fold_in(splits[6], 1), 0, 1).astype(jnp.int32)
    freqs = jnp.clip(jax.random.uniform(splits[7], (BINS,), jnp.float32, 0.1, 3.0), 0.1, 3.0)
    return {"ckpt_e": ckpt_e, "ckpt_h": ckpt_h, "adj_e": adj_e, "adj_h": adj_h, "material": material, "inv_perm": inv_perm, "poling": poling, "freqs": freqs}


COURANT = 0.5
OMEGA = 0.9

def forward_diff(field, axis):
    widths = [(0, 0), (0, 0), (0, 0)]
    widths[axis] = (0, 1)
    padded = jnp.pad(field, widths)
    return lax.slice_in_dim(padded, 1, field.shape[axis] + 1, axis=axis) - field

def backward_diff(field, axis):
    widths = [(0, 0), (0, 0), (0, 0)]
    widths[axis] = (1, 0)
    padded = jnp.pad(field, widths)
    return field - lax.slice_in_dim(padded, 0, field.shape[axis], axis=axis)

def curl_electric(electric):
    comp_x, comp_y, comp_z = (electric[0], electric[1], electric[2])
    return jnp.stack([forward_diff(comp_z, 1) - forward_diff(comp_y, 2), forward_diff(comp_x, 2) - forward_diff(comp_z, 0), forward_diff(comp_y, 0) - forward_diff(comp_x, 1)])

def curl_magnetic(magnetic):
    comp_x, comp_y, comp_z = (magnetic[0], magnetic[1], magnetic[2])
    return jnp.stack([backward_diff(comp_z, 1) - backward_diff(comp_y, 2), backward_diff(comp_x, 2) - backward_diff(comp_z, 0), backward_diff(comp_y, 0) - backward_diff(comp_x, 1)])

def reference(ckpt_e, ckpt_h, adj_e, adj_h, material, inv_perm, poling, freqs):
    inv_eps = jnp.zeros(material.shape, jnp.float32)
    for index in range(NMAT):
        inv_eps = inv_eps + (material == index).astype(jnp.float32) * inv_perm[index]
    chi = (material == 0).astype(jnp.float32)
    signs = (2 * poling - 1).astype(jnp.float32)
    sign_full = jnp.repeat(jnp.repeat(signs, DOMLEN, axis=0), WBLK, axis=1)
    phase = math.pi / DOMLEN * jnp.arange(NX).astype(jnp.float32)
    terms = jnp.stack([sign_full * jnp.cos(phase)[:, None], sign_full * jnp.sin(phase)[:, None]])
    envelope = jnp.cumsum(terms, axis=1) / math.sqrt(NX)
    electric, magnetic = (ckpt_e, ckpt_h)
    stored = []
    for moment in range(STEPS):
        magnetic = magnetic - COURANT * curl_electric(electric)
        electric = electric + COURANT * inv_eps * curl_magnetic(magnetic)
        stored.append(electric)
    adjoint_e, adjoint_h = (adj_e, adj_h)
    gradient = jnp.zeros((2, BINS, NDOM, NWB), jnp.float32)
    scale = 1.0 / math.sqrt(DOMLEN * WBLK * NZ)
    for moment in range(STEPS, 0, -1):
        forward_field = stored[moment - 1]
        drive = envelope[0] * math.cos(OMEGA * moment) + envelope[1] * math.sin(OMEGA * moment)
        adjoint_e = adjoint_e + drive[None, :, :, None] * chi * forward_field
        product = chi * lax.optimization_barrier(jnp.sum(adjoint_e * forward_field, axis=0))
        blocks = product.reshape(NDOM, DOMLEN, NWB, WBLK, NZ).sum(axis=(1, 3, 4)) * scale
        angles = freqs * moment
        gradient = gradient + jnp.stack([jnp.cos(angles)[:, None, None] * blocks, -jnp.sin(angles)[:, None, None] * blocks])
        adjoint_e = adjoint_e - COURANT * inv_eps * curl_magnetic(adjoint_h)
        adjoint_h = adjoint_h + COURANT * curl_electric(adjoint_e)
    return (adjoint_e, adjoint_h, gradient)
```

```python
import functools
import math

import jax
import jax.numpy as jnp
import numpy as np
from jax import lax
from jax.experimental import pallas as pl
from jax.experimental.pallas import tpu as pltpu
from jax.sharding import PartitionSpec as P

STEPS = 8
FIRST = 3
SECOND = STEPS - FIRST
DOM = 8
BINS = 8
OMEGA = 0.9
CELLS = 16
LANES = 128
CHIP = 2 * CELLS

XO, XN, YO, YN = -12, 40, -12, 48
XA, XAN, YA, YAN = -8, 32, -8, 40
YF, YFN = -4, 26

CURL_E = (
    (0, 2, 0, 0), (0, 2, 0, 1), (0, 1, 0, 0),
    (1, 0, 0, 0), (1, 2, 0, 0), (1, 2, 1, 0),
    (2, 1, 0, 0), (2, 1, 1, 0), (2, 0, 0, 0), (2, 0, 0, 1),
)
CURL_H = tuple((o, i, -dx, -dy) for o, i, dx, dy in CURL_E)

MARGIN = 16
SPAN = CELLS + 2 * MARGIN


def own_cells():
    cells = np.zeros((3, SPAN, SPAN), bool)
    cells[:, MARGIN : MARGIN + CELLS, MARGIN : MARGIN + CELLS] = True
    return cells


def reads(target, source, stencil):
    for result, read, dx, dy in stencil:
        target[read] |= np.roll(source[result], (dx, dy), (0, 1))


def box(cells):
    flat = cells.any(0) if cells.ndim == 3 else cells
    xs, ys = (np.flatnonzero(flat.any(1)), np.flatnonzero(flat.any(0)))
    return (int(xs[0]) - MARGIN, int(xs[-1]) + 1 - MARGIN, int(ys[0]) - MARGIN, int(ys[-1]) + 1 - MARGIN)


def adjoint_needs(steps):
    need_e, need_h = own_cells(), own_cells()
    coef = np.zeros((SPAN, SPAN), bool)
    source, box_e, box_h = {}, {}, {}
    for left in range(1, steps + 1):
        box_h[left] = box(need_h)
        electric = need_e.copy()
        reads(electric, need_h, CURL_E)
        before = need_h.copy()
        reads(before, electric, CURL_H)
        coef |= electric.any(0)
        source[left], box_e[left] = electric, box(electric)
        need_e, need_h = electric, before
    return need_e, need_h, coef, source, box_e, box_h


ADJ1 = adjoint_needs(FIRST)
ADJ2 = adjoint_needs(SECOND)


def forward_needs():
    wanted = {n: ADJ2[3][n] for n in range(1, SECOND + 1)}
    wanted.update({n + SECOND: ADJ1[3][n] for n in range(1, FIRST + 1)})
    electric, magnetic = np.zeros((3, SPAN, SPAN), bool), np.zeros((3, SPAN, SPAN), bool)
    coef = ADJ1[2] | ADJ2[2]
    box_e, box_h = {}, {}
    for n in range(STEPS, 0, -1):
        electric |= wanted[n]
        box_e[n] = box(electric)
        coef |= electric.any(0)
        reads(magnetic, electric, CURL_H)
        box_h[n] = box(magnetic)
        reads(electric, magnetic, CURL_E)
    return electric, magnetic, coef, box_e, box_h, {n: box(wanted[n]) for n in wanted}


FWD = forward_needs()


def spans(cells):
    found = {}
    for column in range(SPAN):
        xs = np.flatnonzero(cells[:, column])
        if xs.size:
            found[column - MARGIN] = (int(xs[0]) - MARGIN, int(xs[-1]) + 1 - MARGIN)
    return found


NEEDS1 = [spans(c) for c in (*FWD[0], *FWD[1], FWD[2], *ADJ1[0], *ADJ1[1])]
NEEDS2 = [spans(c) for c in (*ADJ2[0], *ADJ2[1])]


class Message:
    def __init__(self, wanted):
        self.at, rows = {}, 0
        for key in sorted(wanted):
            first, last = wanted[key]
            if last > first:
                self.at[key] = (first, last, rows)
                rows += last - first
        self.rows = rows


class Exchange:
    def __init__(self, needs):
        a0, a1, b0, b1, cr1, cl1, cr2, cl2 = ({} for _ in range(8))
        for f, columns in enumerate(needs):
            for y, (x0, x1) in columns.items():
                if 0 <= y < CELLS:
                    a0[f, y] = (x0, min(x1, 0))
                    a1[f, y] = (CHIP, CELLS + x1)
                    b0[f, y] = (CELLS, x1)
                    b1[f, y] = (CELLS + x0, CELLS)
        for f, columns in enumerate(needs):
            for y, (x0, x1) in columns.items():
                if 0 <= y < CELLS:
                    continue
                first, last = (x0, x1 + CELLS)
                one, two = (cr1, cr2) if y < 0 else (cl1, cl2)
                one[f, y] = (max(first, 0), min(last, CHIP))
                two[f, y, -1] = (first, min(last, 0))
                two[f, y, 1] = (max(first, CHIP), last)
                if y < 0:
                    b0[f, y + CELLS] = (CELLS, max(b0.get((f, y + CELLS), (0, CELLS))[1], min(last, CHIP)))
                else:
                    b1[f, y - CELLS] = (min(b1.get((f, y - CELLS), (CELLS, 0))[0], max(first, 0)), CELLS)
        self.a = (Message(a0), Message(a1))
        self.b = (Message(b0), Message(b1))
        self.c1 = (Message(cl1), Message(cr1))
        self.c2 = (Message(cl2), Message(cr2))
        self.rows = {
            name: -(-max(m.rows for m in getattr(self, name)) // 8) * 8 for name in ("a", "b", "c1", "c2")
        }


EX1 = Exchange(NEEDS1)
EX2 = Exchange(NEEDS2)


def take(message, ref, key, first, last):
    x0, x1, row = message.at[key]
    assert x0 <= first and last <= x1
    return ref[row + first - x0 : row + last - x0, :]


def inside(core, exchange, own, refs, f, y, first, last):
    origins = (
        (-MARGIN, 0, exchange.a[0], "a" if core == 0 else "a_other"),
        (0, CELLS, exchange.b[1], "own" if core == 0 else "b"),
        (CELLS, CHIP, exchange.b[0], "b" if core == 0 else "own"),
        (CHIP, CHIP + MARGIN, exchange.a[1], "a_other" if core == 0 else "a"),
    )
    pieces = []
    for low, high, message, name in origins:
        x0, x1 = (max(first, low), min(last, high))
        if x1 > x0:
            if name == "own":
                pieces.append((x0, x1, own[f, y * CELLS + x0 - low : y * CELLS + x1 - low, :]))
            else:
                pieces.append((x0, x1, take(message, refs[name], (f, y), x0, x1)))
    return pieces


def outside(core, exchange, refs, f, y, first, last):
    receiver = 0 if y >= CELLS else 1
    suffix = "" if receiver == core else "_other"
    pieces = []
    for low, high, name, side in ((-MARGIN, 0, "c2", -1), (0, CHIP, "c1", 0), (CHIP, CHIP + MARGIN, "c2", 1)):
        x0, x1 = (max(first, low), min(last, high))
        if x1 > x0:
            key = (f, y, side) if side else (f, y)
            pieces.append((x0, x1, take(getattr(exchange, name)[receiver], refs[name + suffix], key, x0, x1)))
    return pieces


def put(out, row, x_start, pieces):
    for x0, x1, value in pieces:
        out[row + x0 - x_start : row + x1 - x_start, :] = value


def pack_a(core, exchange, own, out):
    shift = (-CHIP if core == 0 else CHIP) - CELLS * core
    for (f, y), (x0, x1, row) in exchange.a[1 - core].at.items():
        out[row : row + x1 - x0, :] = own[f, y * CELLS + x0 + shift : y * CELLS + x1 + shift, :]


def pack_b(core, exchange, own, out):
    for (f, y), (x0, x1, row) in exchange.b[1 - core].at.items():
        at = y * CELLS - CELLS * core
        out[row : row + x1 - x0, :] = own[f, at + x0 : at + x1, :]


def pack_c(core, exchange, own, refs, name, out):
    shift = CELLS if core == 0 else -CELLS
    for key, (x0, x1, row) in getattr(exchange, name)[1 - core].at.items():
        put(out, row, x0, inside(core, exchange, own, refs, key[0], key[1] + shift, x0, x1))


def unpack(core, exchange, needs, own, refs, store):
    base = CELLS * core
    for f, columns in enumerate(needs):
        for y, (x0, x1) in columns.items():
            if 0 <= y < CELLS:
                pieces = inside(core, exchange, own, refs, f, y, x0 + base, x1 + base)
            else:
                pieces = outside(core, exchange, refs, f, y, x0 + base, x1 + base)
            for first, _, value in pieces:
                store(f, y, first - base, value)


def columns_loop(first, last, vregs, body):
    count = last - first
    trips = max(1, round(count * vregs / 110))
    group = -(-count // trips)
    trips = -(-count // group)
    if trips == 1:
        body(0, group)
        return

    def turn(i, carry):
        body(i * group, group)
        return carry

    lax.fori_loop(0, trips, turn, 0)


def rows_of(span, origin, width):
    x0, x1 = span
    count = min(width, -(-(x1 - x0) // 8) * 8)
    return min(x0, origin + width - count) - origin, count


def magnetic_pass(electric, magnetic, sign, bounds, window):
    x0, x1, y0, y1 = bounds
    xo, xn, yo, _ = window
    offset, count = rows_of((x0, x1), xo, xn)

    def body(start, group):
        last = lax.broadcasted_iota(jnp.int32, (count, LANES), 1) == LANES - 1
        for j in range(group):
            row = (start + (j + y0 - yo)) * xn + offset
            here, up_x, up_y = (pl.ds(row + d, count) for d in (0, 1, xn))
            ex, ey, ez = (electric[c, here, :] for c in range(3))
            ey_z = jnp.where(last, 0.0, pltpu.roll(ey, LANES - 1, 1)) - ey
            ex_z = jnp.where(last, 0.0, pltpu.roll(ex, LANES - 1, 1)) - ex
            curl = (
                (electric[2, up_y, :] - ez) - ey_z,
                ex_z - (electric[2, up_x, :] - ez),
                (electric[1, up_x, :] - ey) - (electric[0, up_y, :] - ex),
            )
            for c in range(3):
                magnetic[c, here, :] = magnetic[c, here, :] + curl[c] if sign > 0 else magnetic[c, here, :] - curl[c]

    columns_loop(y0, y1, count // 8, body)


def electric_pass(magnetic, electric, coef, sign, bounds, window):
    x0, x1, y0, y1 = bounds
    xo, xn, yo, _ = window
    offset, count = rows_of((x0, x1), xo, xn)

    def body(start, group):
        first = lax.broadcasted_iota(jnp.int32, (count, LANES), 1) == 0
        for j in range(group):
            row = (start + (j + y0 - yo)) * xn + offset
            here, down_x, down_y = (pl.ds(row - d, count) for d in (0, 1, xn))
            hx, hy, hz = (magnetic[c, here, :] for c in range(3))
            hy_z = hy - jnp.where(first, 0.0, pltpu.roll(hy, 1, 1))
            hx_z = hx - jnp.where(first, 0.0, pltpu.roll(hx, 1, 1))
            curl = (
                (hz - magnetic[2, down_y, :]) - hy_z,
                hx_z - (hz - magnetic[2, down_x, :]),
                (hy - magnetic[1, down_x, :]) - (hx - magnetic[0, down_y, :]),
            )
            scale = coef[here, :]
            for c in range(3):
                change = scale * curl[c]
                electric[c, here, :] = electric[c, here, :] + change if sign > 0 else electric[c, here, :] - change

    columns_loop(y0, y1, count // 8, body)


def clear_outside(ids, magnetic, bounds, window):
    _, _, y0, y1 = bounds
    xo, xn, yo, _ = window

    @pl.when(ids[1] == 0)
    def _():
        zero = jnp.zeros((y1 - y0, LANES), jnp.float32)
        for c in (1, 2):
            magnetic[c, pl.ds((y0 - yo) * xn - 1 - xo, y1 - y0, stride=xn), :] = zero

    if y0 < 0:

        @pl.when(ids[2] == 0)
        def _():
            zero = jnp.zeros((xn, LANES), jnp.float32)
            for c in (0, 2):
                magnetic[c, (-1 - yo) * xn : -yo * xn, :] = zero


def adjoint_steps(ids, numbers, needs, electric, magnetic, coef, kept, drive, sums, sum_row):
    window = (XA, XAN, YA, YAN)
    for done, n in enumerate(numbers):
        left = len(numbers) - done
        bounds = needs[4][left]
        _, _, y0, y1 = bounds
        field = kept(n)
        for y in range(y0, y1):
            factor = drive[n - 1, y // DOM + 1, :, :]
            at, at_kept = ((y - YA) * XAN, (y - YF) * XAN)
            total = None
            for c in range(3):
                value = field[c, at_kept : at_kept + XAN, :]
                new = electric[c, at : at + XAN, :] + factor * value
                electric[c, at : at + XAN, :] = new
                term = new * value
                total = term if total is None else total + term
            if 0 <= y < CELLS:
                slot = sum_row(n) + (y // DOM) * CELLS
                part = total[-XA : CELLS - XA, :]
                if y % DOM == 0:
                    acc = part
                else:
                    acc = acc + part
                if y % DOM == DOM - 1:
                    sums[slot : slot + CELLS, :] = acc
        electric_pass(magnetic, electric, coef, -1, bounds, window)
        after = needs[5][left]
        magnetic_pass(electric, magnetic, 1, after, window)
        clear_outside(ids, magnetic, after, window)


def both_cores(ids, work):
    for core in (0, 1):

        @pl.when(ids[0] == core)
        def _(core=core):
            work(core)


def kernel_start(ids, poling, e, h, m, ae, ah, own, out_a, out_b, sent, raw, raw_m, arrived):
    loads = [(e, raw.at[0:3]), (h, raw.at[3:6]), (m, raw_m), (ae, raw.at[6:9]), (ah, raw.at[9:12])]
    copies = [pltpu.make_async_copy(source, to, arrived.at[k]) for k, (source, to) in enumerate(loads)]
    for copy in copies:
        copy.start()
    lane = lax.broadcasted_iota(jnp.int32, (8, LANES), 1)
    domain = lane % 32 - 2 * ids[1]
    second = (lane // 32) % 2 == 1
    sign = [jnp.where(second, 2 * poling[d, 1] - 1, 2 * poling[d, 0] - 1).astype(jnp.float32) for d in range(2)]
    before = jnp.where(domain > 0, sign[0], 0.0) - jnp.where(domain > 1, sign[1], 0.0)
    here = jnp.where(domain == 0, sign[0], 0.0) + jnp.where(domain == 1, sign[1], 0.0)
    mine = jnp.where(lane < 64, before, here)
    for k in range(sent.shape[0]):
        sent[k, :, :] = mine
    for k, (first, count) in enumerate(((0, 3), (3, 3), (6, 1), (7, 3), (10, 3))):
        copies[k].wait()
        for f in range(first, first + count):
            for y in range(CELLS):
                rows = pl.ds(y, CELLS, stride=CELLS)
                value = raw_m[rows, :].astype(jnp.float32) + 1.0 if f == 6 else raw[f if f < 6 else f - 1, rows, :]
                own[f, y * CELLS : (y + 1) * CELLS, :] = value

    def work(core):
        pack_a(core, EX1, own, out_a)
        pack_b(core, EX1, own, out_b)

    both_cores(ids, work)


def kernel_c1(exchange, ids, own, b, out):
    both_cores(ids, lambda core: pack_c(core, exchange, own, {"b": b}, "c1", out))


def kernel_c2(exchange, ids, own, a, a_other, *rest):
    out = rest[-1]
    both_cores(ids, lambda core: pack_c(core, exchange, own, {"a": a, "a_other": a_other}, "c2", out))
    if len(rest) == 2:
        rows = exchange.rows["c2"]
        out[rows : rows + 8, :] = rest[0][...]


def drive_tables(ids, env_left, env, env_right, beta, alpha, drive):
    lane = lax.broadcasted_iota(jnp.int32, (8, LANES), 1)
    rows = ((env_left, 1), (env, 0), (env, 1), (env_right, 0))
    for w, (row, which) in enumerate(rows):
        for d in range(4):
            index = jnp.clip(2 * ids[1] + d - 1, 0, 31)
            prefix = jnp.sum(jnp.where(lane == index + 32 * which, row, 0.0), axis=1, keepdims=True)
            sign = jnp.sum(jnp.where(lane == index + 32 * which + 64, row, 0.0), axis=1, keepdims=True)
            prefix = jnp.broadcast_to(prefix, (8, LANES))
            sign = jnp.broadcast_to(sign if d % 2 else -sign, (8, LANES))
            for n in range(STEPS):
                drive[n, w, d * DOM : (d + 1) * DOM, :] = prefix * alpha[n] + sign * beta[n, :, :]


NAMES = ("a", "a_other", "b", "c1", "c1_other", "c2", "c2_other")


def kernel_first(alpha, ids, perm, own, *rest):
    refs = dict(zip(NAMES, rest))
    (env, beta, out_a, out_b, own2, coef_a, kept, sums, drive, ef, hf, mf, coef, ea, ga, late, chi) = rest[len(NAMES) :]

    def store(f, y, x, value):
        count = value.shape[0]
        if f <= 6:
            row = (y - YO) * XN + x - XO
            if f < 3:
                ef[f, row : row + count, :] = value
            elif f < 6:
                hf[f - 3, row : row + count, :] = 2.0 * value
            else:
                mf[row : row + count, :] = value
        else:
            row = (y - YA) * XAN + x - XA
            if f < 10:
                ea[f - 7, row : row + count, :] = value
            else:
                ga[f - 10, row : row + count, :] = 2.0 * value

    both_cores(ids, lambda core: unpack(core, EX1, NEEDS1, own, refs, store))
    env_c, env_d = (refs[k][EX1.rows["c2"] : EX1.rows["c2"] + 8, :] for k in ("c2", "c2_other"))
    left = jnp.where(ids[0] == 0, env_d, env_c)
    right = jnp.where(ids[0] == 0, env_c, env_d)
    drive_tables(ids, left, env[...], right, beta, alpha, drive)

    def coefficients(start, group):
        for j in range(group):
            rows = pl.ds((start + j) * XN, XN)
            index = mf[rows, :]
            value = jnp.zeros((XN, LANES), jnp.float32)
            for k in range(4):
                value = jnp.where(index == float(k + 1), 0.25 * perm[k], value)
            coef[rows, :] = value

    columns_loop(0, YN, XN // 8, coefficients)
    for y in range(YF, YF + YFN):
        at = (y - YO) * XN + XA - XO
        chi[(y - YF) * XAN : (y - YF + 1) * XAN, :] = (mf[at : at + XAN, :] == 1.0).astype(jnp.float32)
    for y in range(YA, YA + 32):
        at = (y - YO) * XN + XA - XO
        coef_a[(y - YA) * XAN : (y - YA + 1) * XAN, :] = coef[at : at + XAN, :]

    window = (XO, XN, YO, YN)
    for n in range(1, STEPS + 1):
        magnetic_pass(ef, hf, -1, FWD[4][n], window)
        clear_outside(ids, hf, FWD[4][n], window)
        electric_pass(hf, ef, coef, 1, FWD[3][n], window)
        _, _, y0, y1 = FWD[5][n]
        target = kept.at[n - 1] if n <= SECOND else late.at[n - 1 - SECOND]

        def keep(start, group, y0=y0, target=target):
            for j in range(group):
                rows = pl.ds((start + (j + y0 - YO)) * XN + XA - XO, XAN)
                to = pl.ds((start + (j + y0 - YF)) * XAN, XAN)
                mask = chi[to, :]
                for k in range(3):
                    target[k, to, :] = ef[k, rows, :] * mask

        for y in range(0, y1 - y0):
            keep(y, 1)

    adjoint_steps(ids, list(range(STEPS, SECOND, -1)), ADJ1, ea, ga, coef_a, lambda n: late.at[n - 1 - SECOND], drive, sums,
                  lambda n: (n - 1 - SECOND) * 2 * CELLS)
    for y in range(CELLS):
        at = (y - YA) * XAN - XA
        for k in range(3):
            own2[k, y * CELLS : (y + 1) * CELLS, :] = ea[k, at : at + CELLS, :]
            own2[k + 3, y * CELLS : (y + 1) * CELLS, :] = ga[k, at : at + CELLS, :]

    def work(core):
        pack_a(core, EX2, own2, out_a)
        pack_b(core, EX2, own2, out_b)

    both_cores(ids, work)


def kernel_second(ids, own, *rest):
    refs = dict(zip(NAMES, rest))
    coef_a, kept, sums1, drive, waves, out_e, out_h, out_g, ea, ga, sums2 = rest[len(NAMES) :]

    def store(f, y, x, value):
        row = (y - YA) * XAN + x - XA
        (ea if f < 3 else ga)[f % 3, row : row + value.shape[0], :] = value

    both_cores(ids, lambda core: unpack(core, EX2, NEEDS2, own, refs, store))
    adjoint_steps(ids, list(range(SECOND, 0, -1)), ADJ2, ea, ga, coef_a, lambda n: kept.at[n - 1], drive, sums2,
                  lambda n: (n - 1) * 2 * CELLS)
    for x in range(CELLS):
        for k in range(3):
            rows = pl.ds(-YA * XAN + x - XA, CELLS, stride=XAN)
            out_e[k, x * CELLS : (x + 1) * CELLS, :] = ea[k, rows, :]
            out_h[k, x * CELLS : (x + 1) * CELLS, :] = 0.5 * ga[k, rows, :]
    total = {(x, w): jnp.zeros((2, BINS), jnp.float32) for x in range(2) for w in range(2)}
    for n in range(1, STEPS + 1):
        ref, base = (sums2, (n - 1) * 2 * CELLS) if n <= SECOND else (sums1, (n - 1 - SECOND) * 2 * CELLS)
        wave = waves[n - 1, :, :]
        for x, w in total:
            at = base + w * CELLS + x * DOM
            part = jnp.sum(ref[at : at + DOM, :], axis=0, keepdims=True)
            total[x, w] = total[x, w] + wave * jnp.sum(part, axis=1, keepdims=True)
    for x, w in total:
        for k in range(2):
            out_g[k, x, w : w + 1, :] = total[x, w][k : k + 1, :]


def call(kernel, name, out_shapes, inputs, smem=1, scratch=(), room=12, hbm=()):
    smem_spec, vmem_spec, hbm_spec = (pl.BlockSpec(memory_space=m) for m in (pltpu.SMEM, pltpu.VMEM, pltpu.HBM))
    return pl.pallas_call(
        kernel,
        out_shape=[jax.ShapeDtypeStruct(s, jnp.float32) for s in out_shapes],
        in_specs=[smem_spec if k < smem else hbm_spec if k in hbm else vmem_spec for k in range(len(inputs))],
        out_specs=[vmem_spec] * len(out_shapes),
        scratch_shapes=[pltpu.VMEM(s, jnp.float32) if isinstance(s, tuple) else s for s in scratch],
        compiler_params=pltpu.CompilerParams(vmem_limit_bytes=room << 20),
        name=name,
    )(*inputs)


def per_device(ckpt_e, ckpt_h, adj_e, adj_h, material, inv_perm, poling, freqs):
    assert material.shape == (CELLS, CELLS, LANES) and poling.shape == (2, 2)
    n_len, n_wid = (lax.axis_size("len"), lax.axis_size("wid"))
    my_len, my_wid = (lax.axis_index("len"), lax.axis_index("wid"))
    ids = jnp.stack([my_len % 2, my_len, my_wid]).astype(jnp.int32)

    def swap(value, axes, pairs):
        return lax.ppermute(value, axes, [p for i, j in pairs for p in ((i, j), (j, i))])

    def swap_a(value):
        return swap(value, "len", [(i, i + 1) for i in range(1, n_len - 1, 2)])

    def swap_b(value):
        return swap(value, "len", [(i, i + 1) for i in range(0, n_len, 2)])

    def swap_c(value):
        pairs = [(i * n_wid + w, (i + 1) * n_wid + w + 1) for i in range(0, n_len, 2) for w in range(n_wid - 1)]
        return swap(value, ("len", "wid"), pairs)

    raw = [x.reshape(3, CELLS * CELLS, LANES) for x in (ckpt_e, ckpt_h)]
    raw += [material.reshape(CELLS * CELLS, LANES)]
    raw += [x.reshape(3, CELLS * CELLS, LANES) for x in (adj_e, adj_h)]

    angle = math.pi / DOM * np.arange(DOM)
    n = np.arange(1, STEPS + 1)
    turn = np.stack([np.cos(OMEGA * n), np.sin(OMEGA * n)], 1)
    norm = 1.0 / math.sqrt(n_len * CELLS)
    partial = np.stack([np.cumsum(np.cos(angle)), np.cumsum(np.sin(angle))], 0)
    beta = jnp.asarray(np.broadcast_to((norm * turn @ partial)[:, :, None], (STEPS, DOM, LANES)), jnp.float32)
    alpha = tuple(float(v) for v in norm * turn @ partial[:, -1])
    phases = freqs[None, :] * jnp.arange(1, STEPS + 1, dtype=jnp.float32)[:, None]
    scale = 1.0 / math.sqrt(DOM * DOM * LANES)
    waves = scale * jnp.stack([jnp.cos(phases), -jnp.sin(phases)], axis=1)

    def spread(exchange, own, a, b, sent=None):
        one = functools.partial(kernel_c1, exchange)
        two = functools.partial(kernel_c2, exchange)
        a, b = (swap_a(a), swap_b(b))
        c1 = swap_c(call(one, "pack_rows", [(exchange.rows["c1"], LANES)], [ids, own, b])[0])
        env, extra = ([], 0)
        if sent is not None:
            sent, b = lax.optimization_barrier((sent, b))
            env, extra = ([jnp.sum(lax.all_to_all(sent, "len", 0, 0), axis=0)], 8)
            a, *env = lax.optimization_barrier((a, *env))
        a_other = swap_b(a)
        c2 = call(two, "pack_corners", [(exchange.rows["c2"] + extra, LANES)], [ids, own, a, a_other, *env])[0]
        c1, c2 = lax.optimization_barrier((c1, c2))
        c2 = swap_c(c2)
        return [a, a_other, b, c1, swap_b(c1), c2, swap_b(c2)], env

    own, a, b, sent = call(
        kernel_start,
        "start",
        [(13, CELLS * CELLS, LANES), (EX1.rows["a"], LANES), (EX1.rows["b"], LANES), (n_len, 8, LANES)],
        [ids, pltpu.with_memory_space_constraint(poling, pltpu.HBM), *[pltpu.with_memory_space_constraint(x, pltpu.HBM) for x in raw]],
        smem=2,
        hbm=range(2, 7),
        scratch=[(12, CELLS * CELLS, LANES), pltpu.VMEM((CELLS * CELLS, LANES), jnp.int32), pltpu.SemaphoreType.DMA((5,))],
    )
    messages, env = spread(EX1, own, a, b, sent)
    a, b, own2, coef_a, kept, sums, drive = call(
        functools.partial(kernel_first, alpha),
        "forward",
        [
            (EX2.rows["a"], LANES),
            (EX2.rows["b"], LANES),
            (6, CELLS * CELLS, LANES),
            (XAN * YAN, LANES),
            (SECOND, 3, YFN * XAN, LANES),
            (FIRST * 2 * CELLS, LANES),
            (STEPS, 4, XAN, LANES),
        ],
        [ids, inv_perm, own, *messages, *env, beta],
        smem=2,
        room=36,
        scratch=[
            (3, XN * YN, LANES),
            (3, XN * YN, LANES),
            (XN * YN, LANES),
            (XN * YN, LANES),
            (3, XAN * YAN, LANES),
            (3, XAN * YAN, LANES),
            (FIRST, 3, YFN * XAN, LANES),
            (YFN * XAN, LANES),
        ],
    )
    messages, _ = spread(EX2, own2, a, b)
    out_e, out_h, out_g = call(
        kernel_second,
        "adjoint",
        [(3, CELLS * CELLS, LANES), (3, CELLS * CELLS, LANES), (2, 2, 2, BINS)],
        [ids, own2, *messages, coef_a, kept, sums, drive, waves],
        room=18,
        scratch=[(3, XAN * YAN, LANES), (3, XAN * YAN, LANES), (SECOND * 2 * CELLS, LANES)],
    )
    shape = (3, CELLS, CELLS, LANES)
    return out_e.reshape(shape), out_h.reshape(shape), out_g.transpose(0, 3, 1, 2)


def solution(mesh):
    field = P(None, "len", "wid", None)
    in_specs = (field, field, field, field, P("len", "wid", None), P(), P("len", "wid"), P())
    out_specs = (field, field, P(None, None, "len", "wid"))
    return jax.shard_map(per_device, mesh=mesh, in_specs=in_specs, out_specs=out_specs, check_vma=False)
```

```python
import functools
import math

import jax
import jax.numpy as jnp
import numpy as np
from jax import lax
from jax.experimental import pallas as pl
from jax.experimental.pallas import tpu as pltpu
from jax.sharding import PartitionSpec as P

STEPS = 8
FIRST = 3
SECOND = STEPS - FIRST
DOM = 8
BINS = 8
OMEGA = 0.9
CELLS = 16
LANES = 128
CHIP = 2 * CELLS

XO, XN, YO, YN = -12, 40, -12, 48
XA, XAN, YA, YAN = -8, 32, -8, 40
YF, YFN = -4, 26

CURL_E = (
    (0, 2, 0, 0), (0, 2, 0, 1), (0, 1, 0, 0),
    (1, 0, 0, 0), (1, 2, 0, 0), (1, 2, 1, 0),
    (2, 1, 0, 0), (2, 1, 1, 0), (2, 0, 0, 0), (2, 0, 0, 1),
)
CURL_H = tuple((o, i, -dx, -dy) for o, i, dx, dy in CURL_E)

MARGIN = 16
SPAN = CELLS + 2 * MARGIN


def own_cells():
    cells = np.zeros((3, SPAN, SPAN), bool)
    cells[:, MARGIN : MARGIN + CELLS, MARGIN : MARGIN + CELLS] = True
    return cells


def reads(target, source, stencil):
    for result, read, dx, dy in stencil:
        target[read] |= np.roll(source[result], (dx, dy), (0, 1))


def box(cells):
    flat = cells.any(0) if cells.ndim == 3 else cells
    xs, ys = (np.flatnonzero(flat.any(1)), np.flatnonzero(flat.any(0)))
    return (int(xs[0]) - MARGIN, int(xs[-1]) + 1 - MARGIN, int(ys[0]) - MARGIN, int(ys[-1]) + 1 - MARGIN)


def adjoint_needs(steps):
    need_e, need_h = own_cells(), own_cells()
    coef = np.zeros((SPAN, SPAN), bool)
    source, box_e, box_h = {}, {}, {}
    for left in range(1, steps + 1):
        box_h[left] = box(need_h)
        electric = need_e.copy()
        reads(electric, need_h, CURL_E)
        before = need_h.copy()
        reads(before, electric, CURL_H)
        coef |= electric.any(0)
        source[left], box_e[left] = electric, box(electric)
        need_e, need_h = electric, before
    return need_e, need_h, coef, source, box_e, box_h


ADJ1 = adjoint_needs(FIRST)
ADJ2 = adjoint_needs(SECOND)


def forward_needs():
    wanted = {n: ADJ2[3][n] for n in range(1, SECOND + 1)}
    wanted.update({n + SECOND: ADJ1[3][n] for n in range(1, FIRST + 1)})
    electric, magnetic = np.zeros((3, SPAN, SPAN), bool), np.zeros((3, SPAN, SPAN), bool)
    coef = ADJ1[2] | ADJ2[2]
    box_e, box_h = {}, {}
    for n in range(STEPS, 0, -1):
        electric |= wanted[n]
        box_e[n] = box(electric)
        coef |= electric.any(0)
        reads(magnetic, electric, CURL_H)
        box_h[n] = box(magnetic)
        reads(electric, magnetic, CURL_E)
    return electric, magnetic, coef, box_e, box_h, {n: box(wanted[n]) for n in wanted}


FWD = forward_needs()


def spans(cells):
    found = {}
    for column in range(SPAN):
        xs = np.flatnonzero(cells[:, column])
        if xs.size:
            found[column - MARGIN] = (int(xs[0]) - MARGIN, int(xs[-1]) + 1 - MARGIN)
    return found


NEEDS1 = [spans(c) for c in (*FWD[0], *FWD[1], FWD[2], *ADJ1[0], *ADJ1[1])]
NEEDS2 = [spans(c) for c in (*ADJ2[0], *ADJ2[1])]


class Message:
    def __init__(self, wanted):
        self.at, rows = {}, 0
        for key in sorted(wanted):
            first, last = wanted[key]
            if last > first:
                self.at[key] = (first, last, rows)
                rows += last - first
        self.rows = rows


class Exchange:
    def __init__(self, needs):
        a0, a1, b0, b1, cr1, cl1, cr2, cl2 = ({} for _ in range(8))
        for f, columns in enumerate(needs):
            for y, (x0, x1) in columns.items():
                if 0 <= y < CELLS:
                    a0[f, y] = (x0, min(x1, 0))
                    a1[f, y] = (CHIP, CELLS + x1)
                    b0[f, y] = (CELLS, x1)
                    b1[f, y] = (CELLS + x0, CELLS)
        for f, columns in enumerate(needs):
            for y, (x0, x1) in columns.items():
                if 0 <= y < CELLS:
                    continue
                first, last = (x0, x1 + CELLS)
                one, two = (cr1, cr2) if y < 0 else (cl1, cl2)
                one[f, y] = (max(first, 0), min(last, CHIP))
                two[f, y, -1] = (first, min(last, 0))
                two[f, y, 1] = (max(first, CHIP), last)
                if y < 0:
                    b0[f, y + CELLS] = (CELLS, max(b0.get((f, y + CELLS), (0, CELLS))[1], min(last, CHIP)))
                else:
                    b1[f, y - CELLS] = (min(b1.get((f, y - CELLS), (CELLS, 0))[0], max(first, 0)), CELLS)
        self.a = (Message(a0), Message(a1))
        self.b = (Message(b0), Message(b1))
        self.c1 = (Message(cl1), Message(cr1))
        self.c2 = (Message(cl2), Message(cr2))
        self.rows = {
            name: -(-max(m.rows for m in getattr(self, name)) // 8) * 8 for name in ("a", "b", "c1", "c2")
        }


EX1 = Exchange(NEEDS1)
EX2 = Exchange(NEEDS2)


def take(message, ref, key, first, last):
    x0, x1, row = message.at[key]
    assert x0 <= first and last <= x1
    return ref[row + first - x0 : row + last - x0, :]


def inside(core, exchange, own, refs, f, y, first, last):
    origins = (
        (-MARGIN, 0, exchange.a[0], "a" if core == 0 else "a_other"),
        (0, CELLS, exchange.b[1], "own" if core == 0 else "b"),
        (CELLS, CHIP, exchange.b[0], "b" if core == 0 else "own"),
        (CHIP, CHIP + MARGIN, exchange.a[1], "a_other" if core == 0 else "a"),
    )
    pieces = []
    for low, high, message, name in origins:
        x0, x1 = (max(first, low), min(last, high))
        if x1 > x0:
            if name == "own":
                pieces.append((x0, x1, own[f, y * CELLS + x0 - low : y * CELLS + x1 - low, :]))
            else:
                pieces.append((x0, x1, take(message, refs[name], (f, y), x0, x1)))
    return pieces


def outside(core, exchange, refs, f, y, first, last):
    receiver = 0 if y >= CELLS else 1
    suffix = "" if receiver == core else "_other"
    pieces = []
    for low, high, name, side in ((-MARGIN, 0, "c2", -1), (0, CHIP, "c1", 0), (CHIP, CHIP + MARGIN, "c2", 1)):
        x0, x1 = (max(first, low), min(last, high))
        if x1 > x0:
            key = (f, y, side) if side else (f, y)
            pieces.append((x0, x1, take(getattr(exchange, name)[receiver], refs[name + suffix], key, x0, x1)))
    return pieces


def put(out, row, x_start, pieces):
    for x0, x1, value in pieces:
        out[row + x0 - x_start : row + x1 - x_start, :] = value


def pack_a(core, exchange, own, out):
    shift = (-CHIP if core == 0 else CHIP) - CELLS * core
    for (f, y), (x0, x1, row) in exchange.a[1 - core].at.items():
        out[row : row + x1 - x0, :] = own[f, y * CELLS + x0 + shift : y * CELLS + x1 + shift, :]


def pack_b(core, exchange, own, out):
    for (f, y), (x0, x1, row) in exchange.b[1 - core].at.items():
        at = y * CELLS - CELLS * core
        out[row : row + x1 - x0, :] = own[f, at + x0 : at + x1, :]


def pack_c(core, exchange, own, refs, name, out):
    shift = CELLS if core == 0 else -CELLS
    for key, (x0, x1, row) in getattr(exchange, name)[1 - core].at.items():
        put(out, row, x0, inside(core, exchange, own, refs, key[0], key[1] + shift, x0, x1))


def unpack(core, exchange, needs, own, refs, store):
    base = CELLS * core
    for f, columns in enumerate(needs):
        for y, (x0, x1) in columns.items():
            if 0 <= y < CELLS:
                pieces = inside(core, exchange, own, refs, f, y, x0 + base, x1 + base)
            else:
                pieces = outside(core, exchange, refs, f, y, x0 + base, x1 + base)
            for first, _, value in pieces:
                store(f, y, first - base, value)


def columns_loop(first, last, vregs, body):
    count = last - first
    trips = max(1, round(count * vregs / 180))
    group = -(-count // trips)
    trips = -(-count // group)
    if trips == 1:
        body(0, group)
        return

    def turn(i, carry):
        body(i * group, group)
        return carry

    lax.fori_loop(0, trips, turn, 0)


def rows_of(span, origin, width):
    x0, x1 = span
    count = min(width, -(-(x1 - x0) // 8) * 8)
    return min(x0, origin + width - count) - origin, count


def magnetic_pass(electric, magnetic, sign, bounds, window):
    x0, x1, y0, y1 = bounds
    xo, xn, yo, _ = window
    offset, count = rows_of((x0, x1), xo, xn)

    def body(start, group):
        last = lax.broadcasted_iota(jnp.int32, (count, LANES), 1) == LANES - 1
        for j in range(group):
            row = (start + (j + y0 - yo)) * xn + offset
            here, up_x, up_y = (pl.ds(row + d, count) for d in (0, 1, xn))
            ex, ey, ez = (electric[c, here, :] for c in range(3))
            ey_z = jnp.where(last, 0.0, pltpu.roll(ey, LANES - 1, 1)) - ey
            ex_z = jnp.where(last, 0.0, pltpu.roll(ex, LANES - 1, 1)) - ex
            curl = (
                (electric[2, up_y, :] - ez) - ey_z,
                ex_z - (electric[2, up_x, :] - ez),
                (electric[1, up_x, :] - ey) - (electric[0, up_y, :] - ex),
            )
            for c in range(3):
                magnetic[c, here, :] = magnetic[c, here, :] + curl[c] if sign > 0 else magnetic[c, here, :] - curl[c]

    columns_loop(y0, y1, count // 8, body)


def electric_pass(magnetic, electric, coef, sign, bounds, window):
    x0, x1, y0, y1 = bounds
    xo, xn, yo, _ = window
    offset, count = rows_of((x0, x1), xo, xn)

    def body(start, group):
        first = lax.broadcasted_iota(jnp.int32, (count, LANES), 1) == 0
        for j in range(group):
            row = (start + (j + y0 - yo)) * xn + offset
            here, down_x, down_y = (pl.ds(row - d, count) for d in (0, 1, xn))
            hx, hy, hz = (magnetic[c, here, :] for c in range(3))
            hy_z = hy - jnp.where(first, 0.0, pltpu.roll(hy, 1, 1))
            hx_z = hx - jnp.where(first, 0.0, pltpu.roll(hx, 1, 1))
            curl = (
                (hz - magnetic[2, down_y, :]) - hy_z,
                hx_z - (hz - magnetic[2, down_x, :]),
                (hy - magnetic[1, down_x, :]) - (hx - magnetic[0, down_y, :]),
            )
            scale = coef[here, :]
            for c in range(3):
                change = scale * curl[c]
                electric[c, here, :] = electric[c, here, :] + change if sign > 0 else electric[c, here, :] - change

    columns_loop(y0, y1, count // 8, body)


def clear_outside(ids, magnetic, bounds, window):
    _, _, y0, y1 = bounds
    xo, xn, yo, _ = window

    @pl.when(ids[1] == 0)
    def _():
        zero = jnp.zeros((y1 - y0, LANES), jnp.float32)
        for c in (1, 2):
            magnetic[c, pl.ds((y0 - yo) * xn - 1 - xo, y1 - y0, stride=xn), :] = zero

    if y0 < 0:

        @pl.when(ids[2] == 0)
        def _():
            zero = jnp.zeros((xn, LANES), jnp.float32)
            for c in (0, 2):
                magnetic[c, (-1 - yo) * xn : -yo * xn, :] = zero


def adjoint_steps(ids, numbers, needs, electric, magnetic, coef, kept, drive, products, sums, sum_row):
    window = (XA, XAN, YA, YAN)
    for done, n in enumerate(numbers):
        left = len(numbers) - done
        x0, x1, y0, y1 = needs[4][left]
        offset, count = rows_of((x0, x1), XA, XAN)
        field = kept(n)
        first = lax.broadcasted_iota(jnp.int32, (count, LANES), 1) == 0
        for y in range(y0, y1):
            row = (y - YA) * XAN + offset
            here, down_x, down_y = (slice(row - d, row - d + count) for d in (0, 1, XAN))
            at = (y - YF) * XAN + offset
            factor = drive[n - 1, y // DOM + 1, offset : offset + count, :]
            values = [field[c, at : at + count, :] for c in range(3)]
            new = [electric[c, here, :] + factor * values[c] for c in range(3)]
            if 0 <= y < CELLS:
                products[y * XAN + offset : y * XAN + offset + count, :] = (
                    new[0] * values[0] + new[1] * values[1] + new[2] * values[2]
                )
            hx, hy, hz = (magnetic[c, here, :] for c in range(3))
            hy_z = hy - jnp.where(first, 0.0, pltpu.roll(hy, 1, 1))
            hx_z = hx - jnp.where(first, 0.0, pltpu.roll(hx, 1, 1))
            curl = (
                (hz - magnetic[2, down_y, :]) - hy_z,
                hx_z - (hz - magnetic[2, down_x, :]),
                (hy - magnetic[1, down_x, :]) - (hx - magnetic[0, down_y, :]),
            )
            scale = coef[here, :]
            for c in range(3):
                electric[c, here, :] = new[c] - scale * curl[c]
        after = needs[5][left]
        magnetic_pass(electric, magnetic, 1, after, window)
        clear_outside(ids, magnetic, after, window)
        for w in range(2):
            total = None
            for y in range(w * DOM, (w + 1) * DOM):
                part = products[y * XAN - XA : y * XAN - XA + CELLS, :]
                total = part if total is None else total + part
            slot = sum_row(n) + w * CELLS
            sums[slot : slot + CELLS, :] = total


def both_cores(ids, work):
    for core in (0, 1):

        @pl.when(ids[0] == core)
        def _(core=core):
            work(core)


def kernel_start(ids, poling, e, h, m, ae, ah, own, out_a, out_b, sent, raw, raw_m, arrived):
    loads = [(e, raw.at[0:3]), (h, raw.at[3:6]), (m, raw_m), (ae, raw.at[6:9]), (ah, raw.at[9:12])]
    copies = [pltpu.make_async_copy(source, to, arrived.at[k]) for k, (source, to) in enumerate(loads)]
    for copy in copies:
        copy.start()
    lane = lax.broadcasted_iota(jnp.int32, (8, LANES), 1)
    domain = lane % 32 - 2 * ids[1]
    second = (lane // 32) % 2 == 1
    sign = [jnp.where(second, 2 * poling[d, 1] - 1, 2 * poling[d, 0] - 1).astype(jnp.float32) for d in range(2)]
    before = jnp.where(domain > 0, sign[0], 0.0) - jnp.where(domain > 1, sign[1], 0.0)
    here = jnp.where(domain == 0, sign[0], 0.0) + jnp.where(domain == 1, sign[1], 0.0)
    mine = jnp.where(lane < 64, before, here)
    for k in range(sent.shape[0]):
        sent[k, :, :] = mine
    for f in range(13):
        if f in (0, 3, 6, 7, 10):
            copies[(0, 3, 6, 7, 10).index(f)].wait()
        for y in range(CELLS):
            rows = pl.ds(y, CELLS, stride=CELLS)
            value = raw_m[rows, :].astype(jnp.float32) + 1.0 if f == 6 else raw[f if f < 6 else f - 1, rows, :]
            own[f, y * CELLS : (y + 1) * CELLS, :] = value

    def work(core):
        pack_a(core, EX1, own, out_a)
        pack_b(core, EX1, own, out_b)

    both_cores(ids, work)


def kernel_c1(exchange, ids, own, b, out):
    both_cores(ids, lambda core: pack_c(core, exchange, own, {"b": b}, "c1", out))


def kernel_c2(exchange, ids, own, a, a_other, *rest):
    out = rest[-1]
    both_cores(ids, lambda core: pack_c(core, exchange, own, {"a": a, "a_other": a_other}, "c2", out))
    if len(rest) == 2:
        rows = exchange.rows["c2"]
        out[rows : rows + 8, :] = rest[0][...]


def drive_tables(ids, env_left, env, env_right, beta, alpha, drive):
    lane = lax.broadcasted_iota(jnp.int32, (8, LANES), 1)
    rows = ((env_left, 1), (env, 0), (env, 1), (env_right, 0))
    for w, (row, which) in enumerate(rows):
        for d in range(4):
            index = jnp.clip(2 * ids[1] + d - 1, 0, 31)
            prefix = jnp.sum(jnp.where(lane == index + 32 * which, row, 0.0), axis=1, keepdims=True)
            sign = jnp.sum(jnp.where(lane == index + 32 * which + 64, row, 0.0), axis=1, keepdims=True)
            prefix = jnp.broadcast_to(prefix, (8, LANES))
            sign = jnp.broadcast_to(sign if d % 2 else -sign, (8, LANES))
            for n in range(STEPS):
                drive[n, w, d * DOM : (d + 1) * DOM, :] = prefix * alpha[n] + sign * beta[n, :, :]


NAMES = ("a", "a_other", "b", "c1", "c1_other", "c2", "c2_other")


def kernel_first(alpha, ids, perm, own, *rest):
    refs = dict(zip(NAMES, rest))
    (env, beta, out_a, out_b, own2, coef_a, kept, sums, drive, ef, hf, mf, coef, ea, ga, late, chi, products) = rest[len(NAMES) :]

    def store(f, y, x, value):
        count = value.shape[0]
        if f <= 6:
            row = (y - YO) * XN + x - XO
            if f < 3:
                ef[f, row : row + count, :] = value
            elif f < 6:
                hf[f - 3, row : row + count, :] = 2.0 * value
            else:
                mf[row : row + count, :] = value
        else:
            row = (y - YA) * XAN + x - XA
            if f < 10:
                ea[f - 7, row : row + count, :] = value
            else:
                ga[f - 10, row : row + count, :] = 2.0 * value

    both_cores(ids, lambda core: unpack(core, EX1, NEEDS1, own, refs, store))
    env_c, env_d = (refs[k][EX1.rows["c2"] : EX1.rows["c2"] + 8, :] for k in ("c2", "c2_other"))
    left = jnp.where(ids[0] == 0, env_d, env_c)
    right = jnp.where(ids[0] == 0, env_c, env_d)
    drive_tables(ids, left, env[...], right, beta, alpha, drive)

    def coefficients(start, group):
        for j in range(group):
            rows = pl.ds((start + j) * XN, XN)
            index = mf[rows, :]
            value = jnp.zeros((XN, LANES), jnp.float32)
            for k in range(4):
                value = jnp.where(index == float(k + 1), 0.25 * perm[k], value)
            coef[rows, :] = value

    columns_loop(0, YN, XN // 8, coefficients)
    for y in range(YF, YF + YFN):
        at = (y - YO) * XN + XA - XO
        chi[(y - YF) * XAN : (y - YF + 1) * XAN, :] = (mf[at : at + XAN, :] == 1.0).astype(jnp.float32)
    for y in range(YA, YA + 32):
        at = (y - YO) * XN + XA - XO
        coef_a[(y - YA) * XAN : (y - YA + 1) * XAN, :] = coef[at : at + XAN, :]

    window = (XO, XN, YO, YN)
    for n in range(1, STEPS + 1):
        magnetic_pass(ef, hf, -1, FWD[4][n], window)
        clear_outside(ids, hf, FWD[4][n], window)
        electric_pass(hf, ef, coef, 1, FWD[3][n], window)
        x0, x1, y0, y1 = FWD[5][n]
        skip, count = rows_of((x0, x1), XA, XAN)
        target = kept.at[n - 1] if n <= SECOND else late.at[n - 1 - SECOND]

        for y in range(y0, y1):
            at, to = ((y - YO) * XN + XA - XO + skip, (y - YF) * XAN + skip)
            mask = chi[to : to + count, :]
            for k in range(3):
                target[k, to : to + count, :] = ef[k, at : at + count, :] * mask

    adjoint_steps(ids, list(range(STEPS, SECOND, -1)), ADJ1, ea, ga, coef_a, lambda n: late.at[n - 1 - SECOND], drive, products, sums,
                  lambda n: (n - 1 - SECOND) * 2 * CELLS)
    for y in range(CELLS):
        at = (y - YA) * XAN - XA
        for k in range(3):
            own2[k, y * CELLS : (y + 1) * CELLS, :] = ea[k, at : at + CELLS, :]
            own2[k + 3, y * CELLS : (y + 1) * CELLS, :] = ga[k, at : at + CELLS, :]

    def work(core):
        pack_a(core, EX2, own2, out_a)
        pack_b(core, EX2, own2, out_b)

    both_cores(ids, work)


def kernel_second(ids, own, *rest):
    refs = dict(zip(NAMES, rest))
    coef_a, kept, sums1, drive, waves, out_e, out_h, out_g, ea, ga, sums2, products = rest[len(NAMES) :]

    def store(f, y, x, value):
        row = (y - YA) * XAN + x - XA
        (ea if f < 3 else ga)[f % 3, row : row + value.shape[0], :] = value

    both_cores(ids, lambda core: unpack(core, EX2, NEEDS2, own, refs, store))
    adjoint_steps(ids, list(range(SECOND, 0, -1)), ADJ2, ea, ga, coef_a, lambda n: kept.at[n - 1], drive, products, sums2,
                  lambda n: (n - 1) * 2 * CELLS)
    for x in range(CELLS):
        for k in range(3):
            rows = pl.ds(-YA * XAN + x - XA, CELLS, stride=XAN)
            out_e[k, x * CELLS : (x + 1) * CELLS, :] = ea[k, rows, :]
            out_h[k, x * CELLS : (x + 1) * CELLS, :] = 0.5 * ga[k, rows, :]
    total = {(x, w): jnp.zeros((2, BINS), jnp.float32) for x in range(2) for w in range(2)}
    for n in range(1, STEPS + 1):
        ref, base = (sums2, (n - 1) * 2 * CELLS) if n <= SECOND else (sums1, (n - 1 - SECOND) * 2 * CELLS)
        wave = waves[n - 1, :, :]
        for x, w in total:
            at = base + w * CELLS + x * DOM
            part = jnp.sum(ref[at : at + DOM, :], axis=0, keepdims=True)
            total[x, w] = total[x, w] + wave * jnp.sum(part, axis=1, keepdims=True)
    for x, w in total:
        for k in range(2):
            out_g[k, x, w : w + 1, :] = total[x, w][k : k + 1, :]


def call(kernel, name, out_shapes, inputs, smem=1, scratch=(), room=12, hbm=()):
    smem_spec, vmem_spec, hbm_spec = (pl.BlockSpec(memory_space=m) for m in (pltpu.SMEM, pltpu.VMEM, pltpu.HBM))
    return pl.pallas_call(
        kernel,
        out_shape=[jax.ShapeDtypeStruct(s, jnp.float32) for s in out_shapes],
        in_specs=[smem_spec if k < smem else hbm_spec if k in hbm else vmem_spec for k in range(len(inputs))],
        out_specs=[vmem_spec] * len(out_shapes),
        scratch_shapes=[pltpu.VMEM(s, jnp.float32) if isinstance(s, tuple) else s for s in scratch],
        compiler_params=pltpu.CompilerParams(vmem_limit_bytes=room << 20),
        name=name,
    )(*inputs)


def per_device(ckpt_e, ckpt_h, adj_e, adj_h, material, inv_perm, poling, freqs):
    assert material.shape == (CELLS, CELLS, LANES) and poling.shape == (2, 2)
    n_len, n_wid = (lax.axis_size("len"), lax.axis_size("wid"))
    my_len, my_wid = (lax.axis_index("len"), lax.axis_index("wid"))
    ids = jnp.stack([my_len % 2, my_len, my_wid]).astype(jnp.int32)

    def swap(value, axes, pairs):
        return lax.ppermute(value, axes, [p for i, j in pairs for p in ((i, j), (j, i))])

    def swap_a(value):
        return swap(value, "len", [(i, i + 1) for i in range(1, n_len - 1, 2)])

    def swap_b(value):
        return swap(value, "len", [(i, i + 1) for i in range(0, n_len, 2)])

    def swap_c(value):
        pairs = [(i * n_wid + w, (i + 1) * n_wid + w + 1) for i in range(0, n_len, 2) for w in range(n_wid - 1)]
        return swap(value, ("len", "wid"), pairs)

    raw = [x.reshape(3, CELLS * CELLS, LANES) for x in (ckpt_e, ckpt_h)]
    raw += [material.reshape(CELLS * CELLS, LANES)]
    raw += [x.reshape(3, CELLS * CELLS, LANES) for x in (adj_e, adj_h)]

    angle = math.pi / DOM * np.arange(DOM)
    n = np.arange(1, STEPS + 1)
    turn = np.stack([np.cos(OMEGA * n), np.sin(OMEGA * n)], 1)
    norm = 1.0 / math.sqrt(n_len * CELLS)
    partial = np.stack([np.cumsum(np.cos(angle)), np.cumsum(np.sin(angle))], 0)
    beta = jnp.asarray(np.broadcast_to((norm * turn @ partial)[:, :, None], (STEPS, DOM, LANES)), jnp.float32)
    alpha = tuple(float(v) for v in norm * turn @ partial[:, -1])
    phases = freqs[None, :] * jnp.arange(1, STEPS + 1, dtype=jnp.float32)[:, None]
    scale = 1.0 / math.sqrt(DOM * DOM * LANES)
    waves = scale * jnp.stack([jnp.cos(phases), -jnp.sin(phases)], axis=1)

    def spread(exchange, own, a, b, sent=None):
        one = functools.partial(kernel_c1, exchange)
        two = functools.partial(kernel_c2, exchange)
        a, b = (swap_a(a), swap_b(b))
        c1 = swap_c(call(one, "pack_rows", [(exchange.rows["c1"], LANES)], [ids, own, b])[0])
        env, extra = ([], 0)
        if sent is not None:
            sent, b = lax.optimization_barrier((sent, b))
            env, extra = ([jnp.sum(lax.all_to_all(sent, "len", 0, 0), axis=0)], 8)
            a, *env = lax.optimization_barrier((a, *env))
        a_other = swap_b(a)
        c2 = call(two, "pack_corners", [(exchange.rows["c2"] + extra, LANES)], [ids, own, a, a_other, *env])[0]
        c1, c2 = lax.optimization_barrier((c1, c2))
        c2 = swap_c(c2)
        return [a, a_other, b, c1, swap_b(c1), c2, swap_b(c2)], env

    own, a, b, sent = call(
        kernel_start,
        "start",
        [(13, CELLS * CELLS, LANES), (EX1.rows["a"], LANES), (EX1.rows["b"], LANES), (n_len, 8, LANES)],
        [ids, pltpu.with_memory_space_constraint(poling, pltpu.HBM), *[pltpu.with_memory_space_constraint(x, pltpu.HBM) for x in raw]],
        smem=2,
        hbm=range(2, 7),
        scratch=[(12, CELLS * CELLS, LANES), pltpu.VMEM((CELLS * CELLS, LANES), jnp.int32), pltpu.SemaphoreType.DMA((5,))],
    )
    messages, env = spread(EX1, own, a, b, sent)
    a, b, own2, coef_a, kept, sums, drive = call(
        functools.partial(kernel_first, alpha),
        "forward",
        [
            (EX2.rows["a"], LANES),
            (EX2.rows["b"], LANES),
            (6, CELLS * CELLS, LANES),
            (XAN * YAN, LANES),
            (SECOND, 3, YFN * XAN, LANES),
            (FIRST * 2 * CELLS, LANES),
            (STEPS, 4, XAN, LANES),
        ],
        [ids, inv_perm, own, *messages, *env, beta],
        smem=2,
        room=36,
        scratch=[
            (3, XN * YN, LANES),
            (3, XN * YN, LANES),
            (XN * YN, LANES),
            (XN * YN, LANES),
            (3, XAN * YAN, LANES),
            (3, XAN * YAN, LANES),
            (FIRST, 3, YFN * XAN, LANES),
            (YFN * XAN, LANES),
            (CELLS * XAN, LANES),
        ],
    )
    messages, _ = spread(EX2, own2, a, b)
    out_e, out_h, out_g = call(
        kernel_second,
        "adjoint",
        [(3, CELLS * CELLS, LANES), (3, CELLS * CELLS, LANES), (2, 2, 2, BINS)],
        [ids, own2, *messages, coef_a, kept, sums, drive, waves],
        room=18,
        scratch=[(3, XAN * YAN, LANES), (3, XAN * YAN, LANES), (SECOND * 2 * CELLS, LANES), (CELLS * XAN, LANES)],
    )
    shape = (3, CELLS, CELLS, LANES)
    return out_e.reshape(shape), out_h.reshape(shape), out_g.transpose(0, 3, 1, 2)


def solution(mesh):
    field = P(None, "len", "wid", None)
    in_specs = (field, field, field, field, P("len", "wid", None), P(), P("len", "wid"), P())
    out_specs = (field, field, P(None, None, "len", "wid"))
    return jax.shard_map(per_device, mesh=mesh, in_specs=in_specs, out_specs=out_specs, check_vma=False)
```

```python
import functools
import math

import jax
import jax.numpy as jnp
import numpy as np
from jax import lax
from jax.experimental import pallas as pl
from jax.experimental.pallas import tpu as pltpu
from jax.sharding import PartitionSpec as P

STEPS = 8
FIRST = 3
SECOND = STEPS - FIRST
DOM = 8
BINS = 8
OMEGA = 0.9
CELLS = 16
LANES = 128
CHIP = 2 * CELLS

XO, XN, YO, YN = -12, 40, -12, 48
XA, XAN, YA, YAN = -8, 32, -8, 40
YF, YFN = -4, 26

CURL_E = (
    (0, 2, 0, 0), (0, 2, 0, 1), (0, 1, 0, 0),
    (1, 0, 0, 0), (1, 2, 0, 0), (1, 2, 1, 0),
    (2, 1, 0, 0), (2, 1, 1, 0), (2, 0, 0, 0), (2, 0, 0, 1),
)
CURL_H = tuple((o, i, -dx, -dy) for o, i, dx, dy in CURL_E)

MARGIN = 16
SPAN = CELLS + 2 * MARGIN


def own_cells():
    cells = np.zeros((3, SPAN, SPAN), bool)
    cells[:, MARGIN : MARGIN + CELLS, MARGIN : MARGIN + CELLS] = True
    return cells


def reads(target, source, stencil):
    for result, read, dx, dy in stencil:
        target[read] |= np.roll(source[result], (dx, dy), (0, 1))


def box(cells):
    flat = cells.any(0) if cells.ndim == 3 else cells
    xs, ys = (np.flatnonzero(flat.any(1)), np.flatnonzero(flat.any(0)))
    return (int(xs[0]) - MARGIN, int(xs[-1]) + 1 - MARGIN, int(ys[0]) - MARGIN, int(ys[-1]) + 1 - MARGIN)


def adjoint_needs(steps):
    need_e, need_h = own_cells(), own_cells()
    coef = np.zeros((SPAN, SPAN), bool)
    source, box_e, box_h = {}, {}, {}
    for left in range(1, steps + 1):
        box_h[left] = box(need_h)
        electric = need_e.copy()
        reads(electric, need_h, CURL_E)
        before = need_h.copy()
        reads(before, electric, CURL_H)
        coef |= electric.any(0)
        source[left], box_e[left] = electric, box(electric)
        need_e, need_h = electric, before
    return need_e, need_h, coef, source, box_e, box_h


ADJ1 = adjoint_needs(FIRST)
ADJ2 = adjoint_needs(SECOND)


def forward_needs():
    wanted = {n: ADJ2[3][n] for n in range(1, SECOND + 1)}
    wanted.update({n + SECOND: ADJ1[3][n] for n in range(1, FIRST + 1)})
    electric, magnetic = np.zeros((3, SPAN, SPAN), bool), np.zeros((3, SPAN, SPAN), bool)
    coef = ADJ1[2] | ADJ2[2]
    box_e, box_h = {}, {}
    for n in range(STEPS, 0, -1):
        electric |= wanted[n]
        box_e[n] = box(electric)
        coef |= electric.any(0)
        reads(magnetic, electric, CURL_H)
        box_h[n] = box(magnetic)
        reads(electric, magnetic, CURL_E)
    return electric, magnetic, coef, box_e, box_h, {n: box(wanted[n]) for n in wanted}


FWD = forward_needs()


def spans(cells):
    found = {}
    for column in range(SPAN):
        xs = np.flatnonzero(cells[:, column])
        if xs.size:
            found[column - MARGIN] = (int(xs[0]) - MARGIN, int(xs[-1]) + 1 - MARGIN)
    return found


NEEDS1 = [spans(c) for c in (*FWD[0], *FWD[1], FWD[2], *ADJ1[0], *ADJ1[1])]
NEEDS2 = [spans(c) for c in (*ADJ2[0], *ADJ2[1])]


class Message:
    def __init__(self, wanted):
        self.at, rows = {}, 0
        for key in sorted(wanted):
            first, last = wanted[key]
            if last > first:
                self.at[key] = (first, last, rows)
                rows += last - first
        self.rows = rows


class Exchange:
    def __init__(self, needs):
        a0, a1, b0, b1, cr1, cl1, cr2, cl2 = ({} for _ in range(8))
        for f, columns in enumerate(needs):
            for y, (x0, x1) in columns.items():
                if 0 <= y < CELLS:
                    a0[f, y] = (x0, min(x1, 0))
                    a1[f, y] = (CHIP, CELLS + x1)
                    b0[f, y] = (CELLS, x1)
                    b1[f, y] = (CELLS + x0, CELLS)
        for f, columns in enumerate(needs):
            for y, (x0, x1) in columns.items():
                if 0 <= y < CELLS:
                    continue
                first, last = (x0, x1 + CELLS)
                one, two = (cr1, cr2) if y < 0 else (cl1, cl2)
                one[f, y] = (max(first, 0), min(last, CHIP))
                two[f, y, -1] = (first, min(last, 0))
                two[f, y, 1] = (max(first, CHIP), last)
                if y < 0:
                    b0[f, y + CELLS] = (CELLS, max(b0.get((f, y + CELLS), (0, CELLS))[1], min(last, CHIP)))
                else:
                    b1[f, y - CELLS] = (min(b1.get((f, y - CELLS), (CELLS, 0))[0], max(first, 0)), CELLS)
        self.a = (Message(a0), Message(a1))
        self.b = (Message(b0), Message(b1))
        self.c1 = (Message(cl1), Message(cr1))
        self.c2 = (Message(cl2), Message(cr2))
        self.rows = {
            name: -(-max(m.rows for m in getattr(self, name)) // 8) * 8 for name in ("a", "b", "c1", "c2")
        }


EX1 = Exchange(NEEDS1)
EX2 = Exchange(NEEDS2)


def take(message, ref, key, first, last):
    x0, x1, row = message.at[key]
    assert x0 <= first and last <= x1
    return ref[row + first - x0 : row + last - x0, :]


def inside(core, exchange, own, refs, f, y, first, last):
    origins = (
        (-MARGIN, 0, exchange.a[0], "a" if core == 0 else "a_other"),
        (0, CELLS, exchange.b[1], "own" if core == 0 else "b"),
        (CELLS, CHIP, exchange.b[0], "b" if core == 0 else "own"),
        (CHIP, CHIP + MARGIN, exchange.a[1], "a_other" if core == 0 else "a"),
    )
    pieces = []
    for low, high, message, name in origins:
        x0, x1 = (max(first, low), min(last, high))
        if x1 > x0:
            if name == "own":
                pieces.append((x0, x1, own[f, y * CELLS + x0 - low : y * CELLS + x1 - low, :]))
            else:
                pieces.append((x0, x1, take(message, refs[name], (f, y), x0, x1)))
    return pieces


def outside(core, exchange, refs, f, y, first, last):
    receiver = 0 if y >= CELLS else 1
    suffix = "" if receiver == core else "_other"
    pieces = []
    for low, high, name, side in ((-MARGIN, 0, "c2", -1), (0, CHIP, "c1", 0), (CHIP, CHIP + MARGIN, "c2", 1)):
        x0, x1 = (max(first, low), min(last, high))
        if x1 > x0:
            key = (f, y, side) if side else (f, y)
            pieces.append((x0, x1, take(getattr(exchange, name)[receiver], refs[name + suffix], key, x0, x1)))
    return pieces


def put(out, row, x_start, pieces):
    for x0, x1, value in pieces:
        out[row + x0 - x_start : row + x1 - x_start, :] = value


def pack_a(core, exchange, own, out):
    shift = (-CHIP if core == 0 else CHIP) - CELLS * core
    for (f, y), (x0, x1, row) in exchange.a[1 - core].at.items():
        out[row : row + x1 - x0, :] = own[f, y * CELLS + x0 + shift : y * CELLS + x1 + shift, :]


def pack_b(core, exchange, own, out):
    for (f, y), (x0, x1, row) in exchange.b[1 - core].at.items():
        at = y * CELLS - CELLS * core
        out[row : row + x1 - x0, :] = own[f, at + x0 : at + x1, :]


def pack_c(core, exchange, own, refs, name, out):
    shift = CELLS if core == 0 else -CELLS
    for key, (x0, x1, row) in getattr(exchange, name)[1 - core].at.items():
        put(out, row, x0, inside(core, exchange, own, refs, key[0], key[1] + shift, x0, x1))


def unpack(core, exchange, needs, own, refs, store):
    base = CELLS * core
    for f, columns in enumerate(needs):
        for y, (x0, x1) in columns.items():
            if 0 <= y < CELLS:
                pieces = inside(core, exchange, own, refs, f, y, x0 + base, x1 + base)
            else:
                pieces = outside(core, exchange, refs, f, y, x0 + base, x1 + base)
            for first, _, value in pieces:
                store(f, y, first - base, value)


def columns_loop(first, last, vregs, body):
    count = last - first
    trips = max(1, round(count * vregs / 180))
    group = -(-count // trips)
    trips = -(-count // group)
    if trips == 1:
        body(0, group)
        return

    def turn(i, carry):
        body(i * group, group)
        return carry

    lax.fori_loop(0, trips, turn, 0)


def rows_of(span, origin, width):
    x0, x1 = span
    count = min(width, -(-(x1 - x0) // 8) * 8)
    return min(x0, origin + width - count) - origin, count


def magnetic_pass(electric, magnetic, sign, bounds, window):
    x0, x1, y0, y1 = bounds
    xo, xn, yo, _ = window
    offset, count = rows_of((x0, x1), xo, xn)

    def body(start, group):
        last = lax.broadcasted_iota(jnp.int32, (count, LANES), 1) == LANES - 1
        for j in range(group):
            row = (start + (j + y0 - yo)) * xn + offset
            here, up_x, up_y = (pl.ds(row + d, count) for d in (0, 1, xn))
            ex, ey, ez = (electric[c, here, :] for c in range(3))
            ey_z = jnp.where(last, 0.0, pltpu.roll(ey, LANES - 1, 1)) - ey
            ex_z = jnp.where(last, 0.0, pltpu.roll(ex, LANES - 1, 1)) - ex
            curl = (
                (electric[2, up_y, :] - ez) - ey_z,
                ex_z - (electric[2, up_x, :] - ez),
                (electric[1, up_x, :] - ey) - (electric[0, up_y, :] - ex),
            )
            for c in range(3):
                magnetic[c, here, :] = magnetic[c, here, :] + curl[c] if sign > 0 else magnetic[c, here, :] - curl[c]

    columns_loop(y0, y1, count // 8, body)


def electric_pass(magnetic, electric, coef, sign, bounds, window):
    x0, x1, y0, y1 = bounds
    xo, xn, yo, _ = window
    offset, count = rows_of((x0, x1), xo, xn)

    def body(start, group):
        first = lax.broadcasted_iota(jnp.int32, (count, LANES), 1) == 0
        for j in range(group):
            row = (start + (j + y0 - yo)) * xn + offset
            here, down_x, down_y = (pl.ds(row - d, count) for d in (0, 1, xn))
            hx, hy, hz = (magnetic[c, here, :] for c in range(3))
            hy_z = hy - jnp.where(first, 0.0, pltpu.roll(hy, 1, 1))
            hx_z = hx - jnp.where(first, 0.0, pltpu.roll(hx, 1, 1))
            curl = (
                (hz - magnetic[2, down_y, :]) - hy_z,
                hx_z - (hz - magnetic[2, down_x, :]),
                (hy - magnetic[1, down_x, :]) - (hx - magnetic[0, down_y, :]),
            )
            scale = coef[here, :]
            for c in range(3):
                change = scale * curl[c]
                electric[c, here, :] = electric[c, here, :] + change if sign > 0 else electric[c, here, :] - change

    columns_loop(y0, y1, count // 8, body)


def clear_outside(ids, magnetic, bounds, window):
    _, _, y0, y1 = bounds
    xo, xn, yo, _ = window

    @pl.when(ids[1] == 0)
    def _():
        zero = jnp.zeros((y1 - y0, LANES), jnp.float32)
        for c in (1, 2):
            magnetic[c, pl.ds((y0 - yo) * xn - 1 - xo, y1 - y0, stride=xn), :] = zero

    if y0 < 0:

        @pl.when(ids[2] == 0)
        def _():
            zero = jnp.zeros((xn, LANES), jnp.float32)
            for c in (0, 2):
                magnetic[c, (-1 - yo) * xn : -yo * xn, :] = zero


def adjoint_steps(ids, numbers, needs, electric, magnetic, coef, kept, drive, products, sums, sum_row):
    window = (XA, XAN, YA, YAN)
    for done, n in enumerate(numbers):
        left = len(numbers) - done
        x0, x1, y0, y1 = needs[4][left]
        offset, count = rows_of((x0, x1), XA, XAN)
        field = kept(n)
        first = lax.broadcasted_iota(jnp.int32, (count, LANES), 1) == 0
        for y in range(y0, y1):
            row = (y - YA) * XAN + offset
            here, down_x, down_y = (slice(row - d, row - d + count) for d in (0, 1, XAN))
            at = (y - YF) * XAN + offset
            factor = drive[n - 1, y // DOM + 1, offset : offset + count, :]
            values = [field[c, at : at + count, :] for c in range(3)]
            new = [electric[c, here, :] + factor * values[c] for c in range(3)]
            if 0 <= y < CELLS:
                products[y * XAN + offset : y * XAN + offset + count, :] = (
                    new[0] * values[0] + new[1] * values[1] + new[2] * values[2]
                )
            hx, hy, hz = (magnetic[c, here, :] for c in range(3))
            hy_z = hy - jnp.where(first, 0.0, pltpu.roll(hy, 1, 1))
            hx_z = hx - jnp.where(first, 0.0, pltpu.roll(hx, 1, 1))
            curl = (
                (hz - magnetic[2, down_y, :]) - hy_z,
                hx_z - (hz - magnetic[2, down_x, :]),
                (hy - magnetic[1, down_x, :]) - (hx - magnetic[0, down_y, :]),
            )
            scale = coef[here, :]
            for c in range(3):
                electric[c, here, :] = new[c] - scale * curl[c]
        after = needs[5][left]
        magnetic_pass(electric, magnetic, 1, after, window)
        clear_outside(ids, magnetic, after, window)
        for w in range(2):
            total = None
            for y in range(w * DOM, (w + 1) * DOM):
                part = products[y * XAN - XA : y * XAN - XA + CELLS, :]
                total = part if total is None else total + part
            slot = sum_row(n) + w * CELLS
            sums[slot : slot + CELLS, :] = total


def both_cores(ids, work):
    for core in (0, 1):

        @pl.when(ids[0] == core)
        def _(core=core):
            work(core)


def kernel_start(ids, poling, e, h, m, ae, ah, own, out_a, out_b, sent, raw, raw_m, arrived):
    loads = [(e, raw.at[0:3]), (h, raw.at[3:6]), (m, raw_m), (ae, raw.at[6:9]), (ah, raw.at[9:12])]
    copies = [pltpu.make_async_copy(source, to, arrived.at[k]) for k, (source, to) in enumerate(loads)]
    for copy in copies:
        copy.start()
    lane = lax.broadcasted_iota(jnp.int32, (8, LANES), 1)
    domain = lane % 32 - 2 * ids[1]
    second = (lane // 32) % 2 == 1
    sign = [jnp.where(second, 2 * poling[d, 1] - 1, 2 * poling[d, 0] - 1).astype(jnp.float32) for d in range(2)]
    before = jnp.where(domain > 0, sign[0], 0.0) - jnp.where(domain > 1, sign[1], 0.0)
    here = jnp.where(domain == 0, sign[0], 0.0) + jnp.where(domain == 1, sign[1], 0.0)
    mine = jnp.where(lane < 64, before, here)
    for k in range(sent.shape[0]):
        sent[k, :, :] = mine[0:1, :]
    for f in range(13):
        if f in (0, 3, 6, 7, 10):
            copies[(0, 3, 6, 7, 10).index(f)].wait()
        for y in range(CELLS):
            rows = pl.ds(y, CELLS, stride=CELLS)
            value = raw_m[rows, :].astype(jnp.float32) + 1.0 if f == 6 else raw[f if f < 6 else f - 1, rows, :]
            own[f, y * CELLS : (y + 1) * CELLS, :] = value

    def work(core):
        pack_a(core, EX1, own, out_a)
        pack_b(core, EX1, own, out_b)

    both_cores(ids, work)


def kernel_c1(exchange, ids, own, b, out):
    both_cores(ids, lambda core: pack_c(core, exchange, own, {"b": b}, "c1", out))


def kernel_c2(exchange, ids, own, a, a_other, *rest):
    out = rest[-1]
    both_cores(ids, lambda core: pack_c(core, exchange, own, {"a": a, "a_other": a_other}, "c2", out))
    if len(rest) == 2:
        rows = exchange.rows["c2"]
        out[rows : rows + 8, :] = jnp.broadcast_to(rest[0][...], (8, LANES))


def drive_tables(ids, env_left, env, env_right, beta, alpha, drive):
    lane = lax.broadcasted_iota(jnp.int32, (8, LANES), 1)
    rows = ((env_left, 1), (env, 0), (env, 1), (env_right, 0))
    for w, (row, which) in enumerate(rows):
        for d in range(4):
            index = jnp.clip(2 * ids[1] + d - 1, 0, 31)
            prefix = jnp.sum(jnp.where(lane == index + 32 * which, row, 0.0), axis=1, keepdims=True)
            sign = jnp.sum(jnp.where(lane == index + 32 * which + 64, row, 0.0), axis=1, keepdims=True)
            prefix = jnp.broadcast_to(prefix, (8, LANES))
            sign = jnp.broadcast_to(sign if d % 2 else -sign, (8, LANES))
            for n in range(STEPS):
                drive[n, w, d * DOM : (d + 1) * DOM, :] = prefix * alpha[n] + sign * beta[n, :, :]


NAMES = ("a", "a_other", "b", "c1", "c1_other", "c2", "c2_other")


def kernel_first(alpha, ids, perm, own, *rest):
    refs = dict(zip(NAMES, rest))
    (env, beta, out_a, out_b, own2, coef_a, kept, sums, drive, ef, hf, mf, coef, ea, ga, late, chi, products) = rest[len(NAMES) :]

    def store(f, y, x, value):
        count = value.shape[0]
        if f <= 6:
            row = (y - YO) * XN + x - XO
            if f < 3:
                ef[f, row : row + count, :] = value
            elif f < 6:
                hf[f - 3, row : row + count, :] = 2.0 * value
            else:
                mf[row : row + count, :] = value
        else:
            row = (y - YA) * XAN + x - XA
            if f < 10:
                ea[f - 7, row : row + count, :] = value
            else:
                ga[f - 10, row : row + count, :] = 2.0 * value

    both_cores(ids, lambda core: unpack(core, EX1, NEEDS1, own, refs, store))
    env_c, env_d = (refs[k][EX1.rows["c2"] : EX1.rows["c2"] + 8, :] for k in ("c2", "c2_other"))
    left = jnp.where(ids[0] == 0, env_d, env_c)
    right = jnp.where(ids[0] == 0, env_c, env_d)
    drive_tables(ids, left, jnp.broadcast_to(env[...], (8, LANES)), right, beta, alpha, drive)

    def coefficients(start, group):
        for j in range(group):
            rows = pl.ds((start + j) * XN, XN)
            index = mf[rows, :]
            value = jnp.zeros((XN, LANES), jnp.float32)
            for k in range(4):
                value = jnp.where(index == float(k + 1), 0.25 * perm[k], value)
            coef[rows, :] = value

    columns_loop(0, YN, XN // 8, coefficients)
    for y in range(YF, YF + YFN):
        at = (y - YO) * XN + XA - XO
        chi[(y - YF) * XAN : (y - YF + 1) * XAN, :] = (mf[at : at + XAN, :] == 1.0).astype(jnp.float32)
    for y in range(YA, YA + 32):
        at = (y - YO) * XN + XA - XO
        coef_a[(y - YA) * XAN : (y - YA + 1) * XAN, :] = coef[at : at + XAN, :]

    window = (XO, XN, YO, YN)
    for n in range(1, STEPS + 1):
        magnetic_pass(ef, hf, -1, FWD[4][n], window)
        clear_outside(ids, hf, FWD[4][n], window)
        electric_pass(hf, ef, coef, 1, FWD[3][n], window)
        x0, x1, y0, y1 = FWD[5][n]
        skip, count = rows_of((x0, x1), XA, XAN)
        target = kept.at[n - 1] if n <= SECOND else late.at[n - 1 - SECOND]

        for y in range(y0, y1):
            at, to = ((y - YO) * XN + XA - XO + skip, (y - YF) * XAN + skip)
            mask = chi[to : to + count, :]
            for k in range(3):
                target[k, to : to + count, :] = ef[k, at : at + count, :] * mask

    adjoint_steps(ids, list(range(STEPS, SECOND, -1)), ADJ1, ea, ga, coef_a, lambda n: late.at[n - 1 - SECOND], drive, products, sums,
                  lambda n: (n - 1 - SECOND) * 2 * CELLS)
    for y in range(CELLS):
        at = (y - YA) * XAN - XA
        for k in range(3):
            own2[k, y * CELLS : (y + 1) * CELLS, :] = ea[k, at : at + CELLS, :]
            own2[k + 3, y * CELLS : (y + 1) * CELLS, :] = ga[k, at : at + CELLS, :]

    def work(core):
        pack_a(core, EX2, own2, out_a)
        pack_b(core, EX2, own2, out_b)

    both_cores(ids, work)


def kernel_second(ids, own, *rest):
    refs = dict(zip(NAMES, rest))
    coef_a, kept, sums1, drive, waves, out_e, out_h, out_g, ea, ga, sums2, products = rest[len(NAMES) :]

    def store(f, y, x, value):
        row = (y - YA) * XAN + x - XA
        (ea if f < 3 else ga)[f % 3, row : row + value.shape[0], :] = value

    both_cores(ids, lambda core: unpack(core, EX2, NEEDS2, own, refs, store))
    adjoint_steps(ids, list(range(SECOND, 0, -1)), ADJ2, ea, ga, coef_a, lambda n: kept.at[n - 1], drive, products, sums2,
                  lambda n: (n - 1) * 2 * CELLS)
    for x in range(CELLS):
        for k in range(3):
            rows = pl.ds(-YA * XAN + x - XA, CELLS, stride=XAN)
            out_e[k, x * CELLS : (x + 1) * CELLS, :] = ea[k, rows, :]
            out_h[k, x * CELLS : (x + 1) * CELLS, :] = 0.5 * ga[k, rows, :]
    total = {(x, w): jnp.zeros((2, BINS), jnp.float32) for x in range(2) for w in range(2)}
    for n in range(1, STEPS + 1):
        ref, base = (sums2, (n - 1) * 2 * CELLS) if n <= SECOND else (sums1, (n - 1 - SECOND) * 2 * CELLS)
        wave = waves[n - 1, :, :]
        for x, w in total:
            at = base + w * CELLS + x * DOM
            part = jnp.sum(ref[at : at + DOM, :], axis=0, keepdims=True)
            total[x, w] = total[x, w] + wave * jnp.sum(part, axis=1, keepdims=True)
    for x, w in total:
        for k in range(2):
            out_g[k, x, w : w + 1, :] = total[x, w][k : k + 1, :]


def call(kernel, name, out_shapes, inputs, smem=1, scratch=(), room=12, hbm=()):
    smem_spec, vmem_spec, hbm_spec = (pl.BlockSpec(memory_space=m) for m in (pltpu.SMEM, pltpu.VMEM, pltpu.HBM))
    return pl.pallas_call(
        kernel,
        out_shape=[jax.ShapeDtypeStruct(s, jnp.float32) for s in out_shapes],
        in_specs=[smem_spec if k < smem else hbm_spec if k in hbm else vmem_spec for k in range(len(inputs))],
        out_specs=[vmem_spec] * len(out_shapes),
        scratch_shapes=[pltpu.VMEM(s, jnp.float32) if isinstance(s, tuple) else s for s in scratch],
        compiler_params=pltpu.CompilerParams(vmem_limit_bytes=room << 20),
        name=name,
    )(*inputs)


def per_device(ckpt_e, ckpt_h, adj_e, adj_h, material, inv_perm, poling, freqs):
    assert material.shape == (CELLS, CELLS, LANES) and poling.shape == (2, 2)
    n_len, n_wid = (lax.axis_size("len"), lax.axis_size("wid"))
    my_len, my_wid = (lax.axis_index("len"), lax.axis_index("wid"))
    ids = jnp.stack([my_len % 2, my_len, my_wid]).astype(jnp.int32)

    def swap(value, axes, pairs):
        return lax.ppermute(value, axes, [p for i, j in pairs for p in ((i, j), (j, i))])

    def swap_a(value):
        return swap(value, "len", [(i, i + 1) for i in range(1, n_len - 1, 2)])

    def swap_b(value):
        return swap(value, "len", [(i, i + 1) for i in range(0, n_len, 2)])

    def swap_c(value):
        pairs = [(i * n_wid + w, (i + 1) * n_wid + w + 1) for i in range(0, n_len, 2) for w in range(n_wid - 1)]
        return swap(value, ("len", "wid"), pairs)

    raw = [x.reshape(3, CELLS * CELLS, LANES) for x in (ckpt_e, ckpt_h)]
    raw += [material.reshape(CELLS * CELLS, LANES)]
    raw += [x.reshape(3, CELLS * CELLS, LANES) for x in (adj_e, adj_h)]

    angle = math.pi / DOM * np.arange(DOM)
    n = np.arange(1, STEPS + 1)
    turn = np.stack([np.cos(OMEGA * n), np.sin(OMEGA * n)], 1)
    norm = 1.0 / math.sqrt(n_len * CELLS)
    partial = np.stack([np.cumsum(np.cos(angle)), np.cumsum(np.sin(angle))], 0)
    beta = jnp.asarray(np.broadcast_to((norm * turn @ partial)[:, :, None], (STEPS, DOM, LANES)), jnp.float32)
    alpha = tuple(float(v) for v in norm * turn @ partial[:, -1])
    phases = freqs[None, :] * jnp.arange(1, STEPS + 1, dtype=jnp.float32)[:, None]
    scale = 1.0 / math.sqrt(DOM * DOM * LANES)
    waves = scale * jnp.stack([jnp.cos(phases), -jnp.sin(phases)], axis=1)

    def spread(exchange, own, a, b, sent=None):
        one = functools.partial(kernel_c1, exchange)
        two = functools.partial(kernel_c2, exchange)
        a, b = (swap_a(a), swap_b(b))
        c1 = swap_c(call(one, "pack_rows", [(exchange.rows["c1"], LANES)], [ids, own, b])[0])
        env, extra = ([], 0)
        if sent is not None:
            sent, b = lax.optimization_barrier((sent, b))
            env, extra = ([jnp.sum(lax.all_to_all(sent, "len", 0, 0), axis=0)], 8)
            a, *env = lax.optimization_barrier((a, *env))
        a_other = swap_b(a)
        c2 = call(two, "pack_corners", [(exchange.rows["c2"] + extra, LANES)], [ids, own, a, a_other, *env])[0]
        c1, c2 = lax.optimization_barrier((c1, c2))
        c2 = swap_c(c2)
        return [a, a_other, b, c1, swap_b(c1), c2, swap_b(c2)], env

    own, a, b, sent = call(
        kernel_start,
        "start",
        [(13, CELLS * CELLS, LANES), (EX1.rows["a"], LANES), (EX1.rows["b"], LANES), (n_len, 1, LANES)],
        [ids, pltpu.with_memory_space_constraint(poling, pltpu.HBM), *[pltpu.with_memory_space_constraint(x, pltpu.HBM) for x in raw]],
        smem=2,
        hbm=range(2, 7),
        scratch=[(12, CELLS * CELLS, LANES), pltpu.VMEM((CELLS * CELLS, LANES), jnp.int32), pltpu.SemaphoreType.DMA((5,))],
    )
    messages, env = spread(EX1, own, a, b, sent)
    a, b, own2, coef_a, kept, sums, drive = call(
        functools.partial(kernel_first, alpha),
        "forward",
        [
            (EX2.rows["a"], LANES),
            (EX2.rows["b"], LANES),
            (6, CELLS * CELLS, LANES),
            (XAN * YAN, LANES),
            (SECOND, 3, YFN * XAN, LANES),
            (FIRST * 2 * CELLS, LANES),
            (STEPS, 4, XAN, LANES),
        ],
        [ids, inv_perm, own, *messages, *env, beta],
        smem=2,
        room=36,
        scratch=[
            (3, XN * YN, LANES),
            (3, XN * YN, LANES),
            (XN * YN, LANES),
            (XN * YN, LANES),
            (3, XAN * YAN, LANES),
            (3, XAN * YAN, LANES),
            (FIRST, 3, YFN * XAN, LANES),
            (YFN * XAN, LANES),
            (CELLS * XAN, LANES),
        ],
    )
    messages, _ = spread(EX2, own2, a, b)
    out_e, out_h, out_g = call(
        kernel_second,
        "adjoint",
        [(3, CELLS * CELLS, LANES), (3, CELLS * CELLS, LANES), (2, 2, 2, BINS)],
        [ids, own2, *messages, coef_a, kept, sums, drive, waves],
        room=18,
        scratch=[(3, XAN * YAN, LANES), (3, XAN * YAN, LANES), (SECOND * 2 * CELLS, LANES), (CELLS * XAN, LANES)],
    )
    shape = (3, CELLS, CELLS, LANES)
    return out_e.reshape(shape), out_h.reshape(shape), out_g.transpose(0, 3, 1, 2)


def solution(mesh):
    field = P(None, "len", "wid", None)
    in_specs = (field, field, field, field, P("len", "wid", None), P(), P("len", "wid"), P())
    out_specs = (field, field, P(None, None, "len", "wid"))
    return jax.shard_map(per_device, mesh=mesh, in_specs=in_specs, out_specs=out_specs, check_vma=False)
```
